256 devices in a mesh: grp: 4 (over y), wide: 4 (over x_hi, core), blk: 16 (over z, x_lo).
Axes of the slice: x: 4 (x_hi: 2, x_lo: 2; x = x_hi * 2 + x_lo), y: 4, z: 8, core: 2. Of those that a mesh axis runs over, the one named last changes fastest.
Arguments:
- activations: bfloat16 [16384, 8192], P('blk', ('grp', 'wide')), may hold values from -6 to 6
- out_grads: bfloat16 [16384, 8192], P('blk', ('grp', 'wide')), may hold values from -6 to 6
- in_projection: bfloat16 [8192, 32], P(('grp', 'wide')), may hold values from -0.0625 to 0.0625
- out_projection: bfloat16 [8192, 64], P(('grp', 'wide')), may hold values from -0.0625 to 0.0625
- in_inverse: float32 [32, 32], replicated, may hold values from -1 to 1
- out_inverse: float32 [64, 64], replicated, may hold values from -0.75 to 0.75
- grad_store: bfloat16 [393216, 2048], P(('grp', 'wide', 'blk')), may hold values from -0.0234375 to 0.0234375
Outputs:
- influence: float32 [512, 393216], P(None, ('grp', 'wide', 'blk'))
The draws below stay inside these ranges and needn't reach their ends.
All inputs are finite; a program needn't handle non-finite values.
Results may differ from the reference program's by a relative error of at most 0.0029.
Values may be sent and summed in bfloat16 or wider, within the bound.
A program may use at most 64 MiB of HBM per device.

```python
import jax
import jax.numpy as jnp
from jax import lax

D = 8192
SEQ = 32
K_IN = 32
K_OUT = 64
QUERIES = 512
TOKENS = 16384
KDIM = 2048
ROWS = 393216


def block_levels(stream_key, shape, split, low, top_value):
    level = 1.0
    for position, parts in split:
        draws = jax.random.uniform(jax.random.fold_in(jax.random.fold_in(stream_key, 6), position), (parts,), jnp.float32, low / len(split), top_value / len(split))
        level = level * jnp.repeat(jnp.exp(draws), shape[position] // parts).reshape((-1,) + (1,) * (len(shape) - 1 - position))
    return level


def normal_values(own_key, extent, width, most, shards=(), kind=jnp.bfloat16):
    loudness = block_levels(own_key, extent, shards, -0.22, 0.18) if shards else 1.0
    entries = jax.random.normal(own_key, extent, jnp.float32) * width * loudness
    return jnp.minimum(jnp.maximum(entries, -most), most).astype(kind)


def setup_inputs(seed: int = 0) -> dict:
    seeds = jax.random.split(jax.random.key(seed), 8)
    activations = normal_values(seeds[0], (TOKENS, D), 1.0, 6.0, ((0, 16), (1, 16)))
    out_grads = normal_values(seeds[1], (TOKENS, D), 1.0, 6.0, ((0, 16), (1, 16)))
    in_projection = normal_values(seeds[2], (D, K_IN), D ** -0.5, 0.0625, ((0, 16),))
    out_projection = normal_values(seeds[3], (D, K_OUT), D ** -0.5, 0.0625, ((0, 16),))
    in_inverse = normal_values(seeds[4], (K_IN, K_IN), K_IN ** -0.5, 1.0, (), jnp.float32)
    out_inverse = normal_values(seeds[5], (K_OUT, K_OUT), K_OUT ** -0.5, 0.75, (), jnp.float32)
    grad_store = normal_values(seeds[6], (ROWS, KDIM), (SEQ * KDIM) ** -0.5, 0.0234375, ((0, 256),))
    return {"activations": activations, "out_grads": out_grads, "in_projection": in_projection, "out_projection": out_projection, "in_inverse": in_inverse, "out_inverse": out_inverse, "grad_store": grad_store}


highest = lax.Precision.HIGHEST


def reference(activations, out_grads, in_projection, out_projection, in_inverse, out_inverse, grad_store):
    low_input = jnp.dot(activations, in_projection, preferred_element_type=jnp.float32)
    low_output = jnp.dot(out_grads, out_projection, preferred_element_type=jnp.float32)
    low_input = low_input.reshape(QUERIES, SEQ, K_IN)
    low_output = low_output.reshape(QUERIES, SEQ, K_OUT)
    gradient = jnp.einsum("qso,qsi->qoi", low_output, low_input, precision=highest)
    shaped = jnp.einsum("ao,qoi->qai", out_inverse, gradient, precision=highest)
    shaped = jnp.einsum("qai,ib->qab", shaped, in_inverse, precision=highest)
    queries = shaped.reshape(QUERIES, KDIM).astype(jnp.bfloat16)
    return lax.dot_general(queries, grad_store, (((1,), (1,)), ((), ())), preferred_element_type=jnp.float32)
```

```python
import functools

import jax
import jax.numpy as jnp
from jax import lax
from jax.experimental import pallas as pl
from jax.experimental.pallas import tpu as pltpu
from jax.sharding import PartitionSpec as P

SEQ = 32
MESH = pl.DeviceIdType.MESH
NT = (((1,), (1,)), ((), ()))
highest = lax.Precision.HIGHEST


def iota(shape, dim):
    return lax.broadcasted_iota(jnp.int32, shape, dim)


def dot32(a, b, dims=(((1,), (0,)), ((), ()))):
    return lax.dot_general(a, b, dims, precision=highest, preferred_element_type=jnp.float32)


def project(act_ref, grd_ref, win_ref, wout_ref, part):
    pairs = 2 * part.shape[0]
    k_in, depth = win_ref.shape
    k_out = wout_ref.shape[0]
    grads = grd_ref[...].reshape(pairs, 2, SEQ, depth)
    wout = wout_ref[...]
    blank = jnp.zeros((k_out, depth), wout.dtype)
    low = None
    for q in range(2):
        weight = jnp.concatenate([wout, blank] if q == 0 else [blank, wout], axis=0)
        rows = grads[:, q].reshape(pairs * SEQ, depth)
        term = lax.dot_general(rows, weight, NT, preferred_element_type=jnp.float32)
        low = term if low is None else low + term
    part[:, :, 0:SEQ, :] = low.reshape(pairs // 2, 2, SEQ, 128)
    acts = act_ref[...].reshape(pairs, 4, SEQ // 2, depth)
    win = win_ref[...]
    blank = jnp.zeros((k_in, depth), win.dtype)
    low = None
    for q in range(4):
        weight = jnp.concatenate([win if j == q else blank for j in range(4)], axis=0)
        rows = acts[:, q].reshape(pairs * SEQ // 2, depth)
        term = lax.dot_general(rows, weight, NT, preferred_element_type=jnp.float32)
        low = term if low is None else low + term
    part[:, :, SEQ:, :] = low.reshape(pairs // 2, 2, SEQ // 2, 128)


def factors(in_inverse, out_inverse):
    k_in, k_out = in_inverse.shape[0], out_inverse.shape[0]
    row, col = iota((128, k_out), 0), iota((128, k_out), 1)
    pick = jnp.where(col == 4 * ((row % 32) // 2) + row // 32, 1.0, 0.0).astype(jnp.float32)
    picked = dot32(pick, out_inverse)
    wide = jnp.concatenate([picked, picked], axis=1)
    row, col = iota((128, 128), 0), iota((128, 128), 1)
    left = jnp.where(col // k_out == row % 2, wide, 0.0)
    tall = jnp.concatenate([in_inverse] * 4, axis=0)
    right = jnp.concatenate([tall] * 4, axis=1)
    return left, right


def shape_queries(low, left, right):
    lo, li = low[:SEQ], low[SEQ:]
    first = dot32(lo[: SEQ // 2], li, (((0,), (0,)), ((), ())))
    second = dot32(lo[SEQ // 2 :], li, (((0,), (0,)), ((), ())))
    row, col = iota((128, 128), 0) // 64, iota((128, 128), 1) // 32
    gradient = jnp.where(col == 2 * row, first, jnp.where(col == 2 * row + 1, second, 0.0))
    both = dot32(left, dot32(gradient, right))
    lane = iota((32, 128), 1) // 32
    out = both[0:32]
    for k in range(1, 4):
        out = jnp.where(lane == k, both[32 * k : 32 * k + 32], out)
    return out


def comm_kernel(
    act_ref, grd_ref, win_ref, wout_ref, in_inv_ref, out_inv_ref,
    q_ref,
    part, from_core, half, from_group, mine,
    send_sem, recv_sem,
):
    y = lax.axis_index("grp")
    w = lax.axis_index("wide")
    b = lax.axis_index("blk")
    ny, nz = 4, 8
    xh, c = w // 2, w % 2
    z, xl = b // 2, b % 2
    x = 2 * xh + xl
    oc = 1 - c

    def device(y_, x_, z_, c_):
        return (y_, 2 * (x_ // 2) + c_, 2 * z_ + x_ % 2)

    group = [(dy, dx) for dy in range(ny) for dx in (0, 2) if (dy, dx) != (0, 0)]
    partner = device(y, x, z, oc)
    to_group = [device((y + dy) % ny, (x + dx) % 4, z, c) for dy, dx in group]
    to_z = [device(y, x, (z + d) % nz, c) for d in range(1, nz)]
    to_x = [device(y, (x + d) % 4, z, c) for d in range(1, 4)]
    to_y = [device((y + d) % ny, x, z, c) for d in range(1, ny)]

    barrier = pltpu.get_barrier_semaphore()
    greeted = [partner] + to_group + to_z + [to_x[0], to_x[2]]
    for peer in greeted:
        pl.semaphore_signal(barrier, inc=1, device_id=peer, device_id_type=MESH)

    project(act_ref, grd_ref, win_ref, wout_ref, part)

    pl.semaphore_wait(barrier, len(greeted))

    used = []

    def copy(src, dst, peer):
        n = len(used)
        used.append(
            pltpu.make_async_remote_copy(
                src_ref=src, dst_ref=dst, send_sem=send_sem.at[n], recv_sem=recv_sem.at[n],
                device_id=peer, device_id_type=MESH,
            )
        )
        return used[-1]

    core = copy(part.at[:, oc], from_core, partner)
    core.start()
    left, right = factors(in_inv_ref[...], out_inv_ref[...])
    core.wait_recv()
    half[...] = part[:, c] + from_core[...]

    sums = []
    for n, (dy, dx) in enumerate(group):
        target = ((y + dy) % ny) * 2 + ((x + dx) % 4) // 2
        sums.append(copy(half.at[target], from_group.at[n], to_group[n]))
        sums[-1].start()
    low = half[y * 2 + xh]
    for n, one in enumerate(sums):
        one.wait_recv()
        low = low + from_group[n]

    rows = shape_queries(low, left, right).astype(jnp.bfloat16)
    for j in range(16):
        mine[j] = rows[2 * j : 2 * j + 2]

    lo_slab, other = 8 * c, 8 * oc
    own = pl.ds(lo_slab, 8)
    swap = copy(mine.at[pl.ds(other, 8)], q_ref.at[pl.ds(other, 8), z, xl, y, xh, c], partner)
    swap.start()
    q_ref[own, z, xl, y, xh, c] = mine[own]
    swap.wait_recv()

    column = q_ref.at[own, z, xl, y, xh]
    stage = [copy(column, column, peer) for peer in to_z]
    for one in stage:
        one.start()
    for one in stage:
        one.wait_recv()

    a, bb = pl.ds(lo_slab, 4), pl.ds(lo_slab + 4, 4)
    a1 = [copy(q_ref.at[a, :, xl, y, xh], q_ref.at[a, :, xl, y, xh], peer) for peer in to_x]
    b1 = [copy(q_ref.at[bb, :, xl, y, xh], q_ref.at[bb, :, xl, y, xh], peer) for peer in to_y]
    for one in a1 + b1:
        one.start()
    for one in a1:
        one.wait_recv()
    a2 = [copy(q_ref.at[a, :, :, y], q_ref.at[a, :, :, y], peer) for peer in to_y]
    for one in a2:
        one.start()
    for one in b1:
        one.wait_recv()
    b2 = [copy(q_ref.at[bb, :, xl, :, xh], q_ref.at[bb, :, xl, :, xh], peer) for peer in to_x]
    for one in b2:
        one.start()
    last = []
    for stage, span in ((a2, a), (b2, bb)):
        for one in stage:
            one.wait_recv()
        last.append(copy(q_ref.at[span], q_ref.at[span], partner))
        last[-1].start()
    for one in last:
        one.wait_recv()
    for one in used:
        one.wait_send()


COPIES = 1 + 7 + 1 + 7 + 3 * 4 + 2


def gather_queries(activations, out_grads, in_projection, out_projection, in_inverse, out_inverse):
    pairs = activations.shape[0] // (2 * SEQ)
    vmem = pl.BlockSpec(memory_space=pltpu.VMEM)
    kern = pl.pallas_call(
        lambda a, g, wi, wo, ii, oi, q, part, fc, *rest: comm_kernel(
            a, g, wi, wo, ii, oi, q, part, fc, *rest
        ),
        out_shape=jax.ShapeDtypeStruct((16, 8, 2, 4, 2, 2, 2, 128), jnp.bfloat16),
        in_specs=[vmem] * 6,
        out_specs=vmem,
        scratch_shapes=[
            pltpu.VMEM((pairs // 2, 2, 48, 128), jnp.float32),
            pltpu.VMEM((pairs // 2, 48, 128), jnp.float32),
            pltpu.VMEM((pairs // 2, 48, 128), jnp.float32),
            pltpu.VMEM((7, 48, 128), jnp.float32),
            pltpu.VMEM((16, 2, 128), jnp.bfloat16),
            pltpu.SemaphoreType.DMA((COPIES,)),
            pltpu.SemaphoreType.DMA((COPIES,)),
        ],
        compiler_params=pltpu.CompilerParams(
            collective_id=0, has_side_effects=True, vmem_limit_bytes=32 * 1024 * 1024
        ),
    )
    return kern(activations, out_grads, in_projection.T, out_projection.T, in_inverse, out_inverse)


def product_kernel(q_ref, s_ref, o_ref):
    queries = jnp.concatenate([q_ref[j] for j in range(16)], axis=1)
    o_ref[...] = lax.dot_general(queries, s_ref[...], NT, preferred_element_type=jnp.float32)


def product(queries, store):
    rows, depth = store.shape
    block = 256
    return pl.pallas_call(
        product_kernel,
        out_shape=jax.ShapeDtypeStruct((512, rows), jnp.float32),
        grid=(rows // block,),
        in_specs=[
            pl.BlockSpec((16, 512, 128), lambda i: (0, 0, 0)),
            pl.BlockSpec((block, depth), lambda i: (i, 0)),
        ],
        out_specs=pl.BlockSpec((512, block), lambda i: (0, i)),
    )(queries, store)


def on_device(
    activations, out_grads, in_projection, out_projection, in_inverse, out_inverse, grad_store
):
    gathered = gather_queries(
        activations, out_grads, in_projection, out_projection, in_inverse, out_inverse
    )
    return product(gathered.reshape(16, 512, 128), grad_store)


def solution(mesh):
    return jax.shard_map(
        on_device,
        mesh=mesh,
        in_specs=(
            P("blk", ("grp", "wide")),
            P("blk", ("grp", "wide")),
            P(("grp", "wide"), None),
            P(("grp", "wide"), None),
            P(),
            P(),
            P(("grp", "wide", "blk"), None),
        ),
        out_specs=P(None, ("grp", "wide", "blk")),
        check_vma=False,
    )
```

```python
import functools

import jax
import jax.numpy as jnp
from jax import lax
from jax.experimental import pallas as pl
from jax.experimental.pallas import tpu as pltpu
from jax.sharding import PartitionSpec as P

SEQ = 32
MESH = pl.DeviceIdType.MESH
NT = (((1,), (1,)), ((), ()))
highest = lax.Precision.HIGHEST


def iota(shape, dim):
    return lax.broadcasted_iota(jnp.int32, shape, dim)


def dot32(a, b, dims=(((1,), (0,)), ((), ()))):
    return lax.dot_general(a, b, dims, precision=highest, preferred_element_type=jnp.float32)


def project(act_ref, grd_ref, win_ref, wout_ref, part, ready_grad, ready_act):
    pairs = 2 * part.shape[0]
    k_in, depth = win_ref.shape
    k_out = wout_ref.shape[0]
    ready_grad()
    grads = grd_ref[...].reshape(pairs, 2, SEQ, depth)
    wout = wout_ref[...]
    blank = jnp.zeros((k_out, depth), wout.dtype)
    low = None
    for q in range(2):
        weight = jnp.concatenate([wout, blank] if q == 0 else [blank, wout], axis=0)
        rows = grads[:, q].reshape(pairs * SEQ, depth)
        term = lax.dot_general(rows, weight, NT, preferred_element_type=jnp.float32)
        low = term if low is None else low + term
    part[:, :, 0:SEQ, :] = low.reshape(pairs // 2, 2, SEQ, 128)
    ready_act()
    acts = act_ref[...].reshape(pairs, 4, SEQ // 2, depth)
    win = win_ref[...]
    blank = jnp.zeros((k_in, depth), win.dtype)
    low = None
    for q in range(4):
        weight = jnp.concatenate([win if j == q else blank for j in range(4)], axis=0)
        rows = acts[:, q].reshape(pairs * SEQ // 2, depth)
        term = lax.dot_general(rows, weight, NT, preferred_element_type=jnp.float32)
        low = term if low is None else low + term
    part[:, :, SEQ:, :] = low.reshape(pairs // 2, 2, SEQ // 2, 128)


def factors(in_inverse, out_inverse):
    k_in, k_out = in_inverse.shape[0], out_inverse.shape[0]
    row, col = iota((128, k_out), 0), iota((128, k_out), 1)
    pick = jnp.where(col == 4 * ((row % 32) // 2) + row // 32, 1.0, 0.0).astype(jnp.float32)
    picked = dot32(pick, out_inverse)
    wide = jnp.concatenate([picked, picked], axis=1)
    row, col = iota((128, 128), 0), iota((128, 128), 1)
    left = jnp.where(col // k_out == row % 2, wide, 0.0)
    tall = jnp.concatenate([in_inverse] * 4, axis=0)
    right = jnp.concatenate([tall] * 4, axis=1)
    return left, right


def shape_queries(low, left, right):
    lo, li = low[:SEQ], low[SEQ:]
    first = dot32(lo[: SEQ // 2], li, (((0,), (0,)), ((), ())))
    second = dot32(lo[SEQ // 2 :], li, (((0,), (0,)), ((), ())))
    row, col = iota((128, 128), 0) // 64, iota((128, 128), 1) // 32
    gradient = jnp.where(col == 2 * row, first, jnp.where(col == 2 * row + 1, second, 0.0))
    both = dot32(left, dot32(gradient, right))
    lane = iota((32, 128), 1) // 32
    out = both[0:32]
    for k in range(1, 4):
        out = jnp.where(lane == k, both[32 * k : 32 * k + 32], out)
    return out


def comm_kernel(
    act_hbm, grd_hbm, win_hbm, wout_hbm, in_inv_hbm, out_inv_hbm,
    q_ref,
    act_ref, grd_ref, win_ref, wout_ref, in_inv_ref, out_inv_ref,
    part, from_core, half, from_group, mine,
    load_sem, send_sem, recv_sem,
):
    loads = [
        pltpu.make_async_copy(src, dst, load_sem.at[n])
        for n, (src, dst) in enumerate((
            (wout_hbm, wout_ref), (grd_hbm, grd_ref), (win_hbm, win_ref), (act_hbm, act_ref),
            (in_inv_hbm, in_inv_ref), (out_inv_hbm, out_inv_ref),
        ))
    ]
    for one in loads:
        one.start()

    y = lax.axis_index("grp")
    w = lax.axis_index("wide")
    b = lax.axis_index("blk")
    ny, nz = 4, 8
    xh, c = w // 2, w % 2
    z, xl = b // 2, b % 2
    x = 2 * xh + xl
    oc = 1 - c

    def device(y_, x_, z_, c_):
        return (y_, 2 * (x_ // 2) + c_, 2 * z_ + x_ % 2)

    group = [(dy, dx) for dy in range(ny) for dx in (0, 2) if (dy, dx) != (0, 0)]
    partner = device(y, x, z, oc)
    to_group = [device((y + dy) % ny, (x + dx) % 4, z, c) for dy, dx in group]
    to_z = [device(y, x, (z + d) % nz, c) for d in range(1, nz)]
    to_x = [device(y, (x + d) % 4, z, c) for d in range(1, 4)]
    to_y = [device((y + d) % ny, x, z, c) for d in range(1, ny)]

    barrier = pltpu.get_barrier_semaphore()
    greeted = [partner] + to_group + to_z + [to_x[0], to_x[2]]
    for peer in greeted:
        pl.semaphore_signal(barrier, inc=1, device_id=peer, device_id_type=MESH)

    def arrived(first, stop):
        for one in loads[first:stop]:
            one.wait()

    project(
        act_ref, grd_ref, win_ref, wout_ref, part, lambda: arrived(0, 2), lambda: arrived(2, 4)
    )
    arrived(4, 6)

    pl.semaphore_wait(barrier, len(greeted))

    used = []

    def copy(src, dst, peer):
        n = len(used)
        used.append(
            pltpu.make_async_remote_copy(
                src_ref=src, dst_ref=dst, send_sem=send_sem.at[n], recv_sem=recv_sem.at[n],
                device_id=peer, device_id_type=MESH,
            )
        )
        return used[-1]

    core = copy(part.at[:, oc], from_core, partner)
    core.start()
    left, right = factors(in_inv_ref[...], out_inv_ref[...])
    core.wait_recv()
    half[...] = part[:, c] + from_core[...]

    sums = []
    for n, (dy, dx) in enumerate(group):
        target = ((y + dy) % ny) * 2 + ((x + dx) % 4) // 2
        sums.append(copy(half.at[target], from_group.at[n], to_group[n]))
        sums[-1].start()
    low = half[y * 2 + xh]
    for n, one in enumerate(sums):
        one.wait_recv()
        low = low + from_group[n]

    rows = shape_queries(low, left, right).astype(jnp.bfloat16)
    for j in range(16):
        mine[j] = rows[2 * j : 2 * j + 2]

    lo_slab, other = 8 * c, 8 * oc
    own = pl.ds(lo_slab, 8)
    swap = copy(mine.at[pl.ds(other, 8)], q_ref.at[pl.ds(other, 8), z, xl, y, xh, c], partner)
    swap.start()
    q_ref[own, z, xl, y, xh, c] = mine[own]
    swap.wait_recv()

    column = q_ref.at[own, z, xl, y, xh]
    stage = [copy(column, column, peer) for peer in to_z]
    for one in stage:
        one.start()
    for one in stage:
        one.wait_recv()

    a, bb = pl.ds(lo_slab, 4), pl.ds(lo_slab + 4, 4)
    a1 = [copy(q_ref.at[a, :, xl, y, xh], q_ref.at[a, :, xl, y, xh], peer) for peer in to_x]
    b1 = [copy(q_ref.at[bb, :, xl, y, xh], q_ref.at[bb, :, xl, y, xh], peer) for peer in to_y]
    for one in a1 + b1:
        one.start()
    for one in a1:
        one.wait_recv()
    a2 = [copy(q_ref.at[a, :, :, y], q_ref.at[a, :, :, y], peer) for peer in to_y]
    for one in a2:
        one.start()
    for one in b1:
        one.wait_recv()
    b2 = [copy(q_ref.at[bb, :, xl, :, xh], q_ref.at[bb, :, xl, :, xh], peer) for peer in to_x]
    for one in b2:
        one.start()
    last = []
    for stage, span in ((a2, a), (b2, bb)):
        for one in stage:
            one.wait_recv()
        last.append(copy(q_ref.at[span], q_ref.at[span], partner))
        last[-1].start()
    for one in last:
        one.wait_recv()
    for one in used:
        one.wait_send()


COPIES = 1 + 7 + 1 + 7 + 3 * 4 + 2


def gather_queries(activations, out_grads, in_projection, out_projection, in_inverse, out_inverse):
    pairs = activations.shape[0] // (2 * SEQ)
    operands = (
        activations, out_grads, in_projection.T, out_projection.T, in_inverse, out_inverse
    )
    kern = pl.pallas_call(
        comm_kernel,
        out_shape=jax.ShapeDtypeStruct((16, 8, 2, 4, 2, 2, 2, 128), jnp.bfloat16),
        in_specs=[pl.BlockSpec(memory_space=pl.ANY)] * len(operands),
        out_specs=pl.BlockSpec(memory_space=pltpu.VMEM),
        scratch_shapes=[
            *[pltpu.VMEM(one.shape, one.dtype) for one in operands],
            pltpu.VMEM((pairs // 2, 2, 48, 128), jnp.float32),
            pltpu.VMEM((pairs // 2, 48, 128), jnp.float32),
            pltpu.VMEM((pairs // 2, 48, 128), jnp.float32),
            pltpu.VMEM((7, 48, 128), jnp.float32),
            pltpu.VMEM((16, 2, 128), jnp.bfloat16),
            pltpu.SemaphoreType.DMA((len(operands),)),
            pltpu.SemaphoreType.DMA((COPIES,)),
            pltpu.SemaphoreType.DMA((COPIES,)),
        ],
        compiler_params=pltpu.CompilerParams(
            collective_id=0, has_side_effects=True, vmem_limit_bytes=60 * 1024 * 1024
        ),
    )
    return kern(*operands)


def product_kernel(q_ref, s_ref, o_ref):
    queries = jnp.concatenate([q_ref[j] for j in range(16)], axis=1)
    o_ref[...] = lax.dot_general(queries, s_ref[...], NT, preferred_element_type=jnp.float32)


def product(queries, store):
    rows, depth = store.shape
    block = 256
    return pl.pallas_call(
        product_kernel,
        out_shape=jax.ShapeDtypeStruct((512, rows), jnp.float32),
        grid=(rows // block,),
        in_specs=[
            pl.BlockSpec((16, 512, 128), lambda i: (0, 0, 0)),
            pl.BlockSpec((block, depth), lambda i: (i, 0)),
        ],
        out_specs=pl.BlockSpec((512, block), lambda i: (0, i)),
    )(queries, store)


def on_device(
    activations, out_grads, in_projection, out_projection, in_inverse, out_inverse, grad_store
):
    gathered = gather_queries(
        activations, out_grads, in_projection, out_projection, in_inverse, out_inverse
    )
    return product(gathered.reshape(16, 512, 128), grad_store)


def solution(mesh):
    return jax.shard_map(
        on_device,
        mesh=mesh,
        in_specs=(
            P("blk", ("grp", "wide")),
            P("blk", ("grp", "wide")),
            P(("grp", "wide"), None),
            P(("grp", "wide"), None),
            P(),
            P(),
            P(("grp", "wide", "blk"), None),
        ),
        out_specs=P(None, ("grp", "wide", "blk")),
        check_vma=False,
    )
```

```python
import functools

import jax
import jax.numpy as jnp
from jax import lax
from jax.experimental import pallas as pl
from jax.experimental.pallas import tpu as pltpu
from jax.sharding import PartitionSpec as P

SEQ = 32
MESH = pl.DeviceIdType.MESH
NT = (((1,), (1,)), ((), ()))
highest = lax.Precision.HIGHEST


def iota(shape, dim):
    return lax.broadcasted_iota(jnp.int32, shape, dim)


def dot32(a, b, dims=(((1,), (0,)), ((), ()))):
    return lax.dot_general(a, b, dims, precision=highest, preferred_element_type=jnp.float32)


def project(act_ref, grd_ref, win_ref, wout_ref, part, ready_grad, ready_act):
    pairs = 2 * part.shape[0]
    k_in, depth = win_ref.shape
    k_out = wout_ref.shape[0]
    ready_grad()
    grads = grd_ref[...].reshape(pairs, 2, SEQ, depth)
    wout = wout_ref[...]
    blank = jnp.zeros((k_out, depth), wout.dtype)
    low = None
    for q in range(2):
        weight = jnp.concatenate([wout, blank] if q == 0 else [blank, wout], axis=0)
        rows = grads[:, q].reshape(pairs * SEQ, depth)
        term = lax.dot_general(rows, weight, NT, preferred_element_type=jnp.float32)
        low = term if low is None else low + term
    part[:, :, 0:SEQ, :] = low.reshape(pairs // 2, 2, SEQ, 128)
    ready_act()
    acts = act_ref[...].reshape(pairs, 4, SEQ // 2, depth)
    win = win_ref[...]
    blank = jnp.zeros((k_in, depth), win.dtype)
    low = None
    for q in range(4):
        weight = jnp.concatenate([win if j == q else blank for j in range(4)], axis=0)
        rows = acts[:, q].reshape(pairs * SEQ // 2, depth)
        term = lax.dot_general(rows, weight, NT, preferred_element_type=jnp.float32)
        low = term if low is None else low + term
    part[:, :, SEQ:, :] = low.reshape(pairs // 2, 2, SEQ // 2, 128)


def factors(in_inverse, out_inverse):
    k_in, k_out = in_inverse.shape[0], out_inverse.shape[0]
    row, col = iota((128, k_out), 0), iota((128, k_out), 1)
    pick = jnp.where(col == 4 * ((row % 32) // 2) + row // 32, 1.0, 0.0).astype(jnp.float32)
    picked = dot32(pick, out_inverse)
    wide = jnp.concatenate([picked, picked], axis=1)
    row, col = iota((128, 128), 0), iota((128, 128), 1)
    left = jnp.where(col // k_out == row % 2, wide, 0.0)
    tall = jnp.concatenate([in_inverse] * 4, axis=0)
    right = jnp.concatenate([tall] * 4, axis=1)
    return left, right


def shape_queries(low, left, right):
    lo, li = low[:SEQ], low[SEQ:]
    first = dot32(lo[: SEQ // 2], li, (((0,), (0,)), ((), ())))
    second = dot32(lo[SEQ // 2 :], li, (((0,), (0,)), ((), ())))
    row, col = iota((128, 128), 0) // 64, iota((128, 128), 1) // 32
    gradient = jnp.where(col == 2 * row, first, jnp.where(col == 2 * row + 1, second, 0.0))
    both = dot32(left, dot32(gradient, right))
    lane = iota((32, 128), 1) // 32
    out = both[0:32]
    for k in range(1, 4):
        out = jnp.where(lane == k, both[32 * k : 32 * k + 32], out)
    return out


def influence_kernel(
    act_hbm, grd_hbm, win_hbm, wout_hbm, in_inv_hbm, out_inv_hbm, store_hbm,
    out_ref,
    act_ref, grd_ref, win_ref, wout_ref, in_inv_ref, out_inv_ref, store,
    part, from_core, half, from_group, mine, queries,
    load_sem, send_sem, recv_sem,
):
    loads = [
        pltpu.make_async_copy(src, dst, load_sem.at[n])
        for n, (src, dst) in enumerate((
            (wout_hbm, wout_ref), (grd_hbm, grd_ref), (win_hbm, win_ref), (act_hbm, act_ref),
            (in_inv_hbm, in_inv_ref), (out_inv_hbm, out_inv_ref),
        ))
    ]
    for one in loads:
        one.start()

    y = lax.axis_index("grp")
    w = lax.axis_index("wide")
    b = lax.axis_index("blk")
    ny, nz = 4, 8
    xh, c = w // 2, w % 2
    z, xl = b // 2, b % 2
    x = 2 * xh + xl
    oc = 1 - c

    def device(y_, x_, z_, c_):
        return (y_, 2 * (x_ // 2) + c_, 2 * z_ + x_ % 2)

    group = [(dy, dx) for dy in range(ny) for dx in (0, 2) if (dy, dx) != (0, 0)]
    partner = device(y, x, z, oc)
    to_group = [device((y + dy) % ny, (x + dx) % 4, z, c) for dy, dx in group]
    to_z = [device(y, x, (z + d) % nz, c) for d in range(1, nz)]
    to_x = [device(y, (x + d) % 4, z, c) for d in range(1, 4)]
    to_y = [device((y + d) % ny, x, z, c) for d in range(1, ny)]

    barrier = pltpu.get_barrier_semaphore()
    greeted = [partner] + to_group + to_z + [to_x[0], to_x[2]]
    for peer in greeted:
        pl.semaphore_signal(barrier, inc=1, device_id=peer, device_id_type=MESH)

    def arrived(first, stop):
        for one in loads[first:stop]:
            one.wait()

    project(
        act_ref, grd_ref, win_ref, wout_ref, part, lambda: arrived(0, 2), lambda: arrived(2, 4)
    )
    arrived(4, 6)
    load_store = pltpu.make_async_copy(store_hbm, store, load_sem.at[len(loads)])
    load_store.start()

    pl.semaphore_wait(barrier, len(greeted))

    used = []

    def copy(src, dst, peer):
        n = len(used)
        used.append(
            pltpu.make_async_remote_copy(
                src_ref=src, dst_ref=dst, send_sem=send_sem.at[n], recv_sem=recv_sem.at[n],
                device_id=peer, device_id_type=MESH,
            )
        )
        return used[-1]

    core = copy(part.at[:, oc], from_core, partner)
    core.start()
    left, right = factors(in_inv_ref[...], out_inv_ref[...])
    core.wait_recv()
    half[...] = part[:, c] + from_core[...]

    sums = []
    for n, (dy, dx) in enumerate(group):
        target = ((y + dy) % ny) * 2 + ((x + dx) % 4) // 2
        sums.append(copy(half.at[target], from_group.at[n], to_group[n]))
        sums[-1].start()
    low = half[y * 2 + xh]
    for n, one in enumerate(sums):
        one.wait_recv()
        low = low + from_group[n]

    rows = shape_queries(low, left, right).astype(jnp.bfloat16)
    for j in range(16):
        mine[j] = rows[2 * j : 2 * j + 2]

    base, other = 8 * c, 8 * oc
    own = pl.ds(base, 8)
    swap = copy(mine.at[pl.ds(other, 8)], queries.at[pl.ds(other, 8), z, xl, y, xh, c], partner)
    swap.start()
    queries[own, z, xl, y, xh, c] = mine[own]
    swap.wait_recv()

    def send(view, peers):
        sent = [copy(view, view, peer) for peer in peers]
        for one in sent:
            one.start()
        return sent

    def arrive(sent):
        for one in sent:
            one.wait_recv()

    def line(s, x_, y_):
        return (
            queries.at[base + 2 * s, :, x_ % 2, y, x_ // 2],
            queries.at[base + 2 * s + 1, :, xl, y_, xh],
        )

    def plane(s, x_, y_):
        return (
            queries.at[base + 2 * s, :, :, y_],
            queries.at[base + 2 * s + 1, :, x_ % 2, :, x_ // 2],
        )

    CHUNKS = 4
    columns = [send(queries.at[pl.ds(base, 2), z, xl, y, xh], to_z)]
    columns.append(send(queries.at[pl.ds(base + 2, 6), z, xl, y, xh], to_z))
    lines = []
    for s in range(CHUNKS):
        if s < 2:
            arrive(columns[s])
        along_x, along_y = line(s, x, y)
        lines.append(send(along_x, to_x) + send(along_y, to_y))
    planes = []
    for s in range(CHUNKS):
        arrive(lines[s])
        along_y, along_x = plane(s, x, y)
        planes.append(
            send(along_y, [to_y[0], to_y[2]]) + send(along_x, [to_x[0], to_x[2]])
        )
    passed = []
    for s in range(CHUNKS):
        arrive(planes[s])
        step, ahead = (3, 0) if s % 2 == 0 else (1, 2)
        along_y, along_x = plane(s, (x + step) % 4, (y + step) % 4)
        passed.append(send(along_y, [to_y[ahead]]) + send(along_x, [to_x[ahead]]))

    view = queries.reshape(16, 512, 128)

    def add_product(slab, first):
        rows = jnp.concatenate([view[slab], view[slab + 1]], axis=1)
        column = pl.ds(pl.multiple_of(slab * 128, 256), 256)

        def tile(n, _):
            part_rows = pl.ds(pl.multiple_of(n * 256, 256), 256)
            term = lax.dot_general(
                rows, store[part_rows, column], NT, preferred_element_type=jnp.float32
            )
            if first:
                out_ref[:, part_rows] = term
            else:
                out_ref[:, part_rows] += term
            return 0

        lax.fori_loop(0, store.shape[0] // 256, tile, 0)

    load_store.wait()
    swaps = []
    for s in range(CHUNKS):
        arrive(passed[s])
        swaps.append(send(queries.at[pl.ds(base + 2 * s, 2)], [partner]))
        add_product(base + 2 * s, s == 0)
    for s in range(CHUNKS):
        arrive(swaps[s])
        add_product(other + 2 * s, False)
    for one in used:
        one.wait_send()


COPIES = 1 + 7 + 1 + 2 * 7 + 4 * (6 + 4 + 2 + 1)


def on_device(
    activations, out_grads, in_projection, out_projection, in_inverse, out_inverse, grad_store
):
    pairs = activations.shape[0] // (2 * SEQ)
    operands = (
        activations, out_grads, in_projection.T, out_projection.T, in_inverse, out_inverse,
        grad_store,
    )
    kern = pl.pallas_call(
        influence_kernel,
        out_shape=jax.ShapeDtypeStruct((512, grad_store.shape[0]), jnp.float32),
        in_specs=[pl.BlockSpec(memory_space=pl.ANY)] * len(operands),
        out_specs=pl.BlockSpec(memory_space=pltpu.VMEM),
        scratch_shapes=[
            *[pltpu.VMEM(one.shape, one.dtype) for one in operands],
            pltpu.VMEM((pairs // 2, 2, 48, 128), jnp.float32),
            pltpu.VMEM((pairs // 2, 48, 128), jnp.float32),
            pltpu.VMEM((pairs // 2, 48, 128), jnp.float32),
            pltpu.VMEM((7, 48, 128), jnp.float32),
            pltpu.VMEM((16, 2, 128), jnp.bfloat16),
            pltpu.VMEM((16, 8, 2, 4, 2, 2, 2, 128), jnp.bfloat16),
            pltpu.SemaphoreType.DMA((len(operands),)),
            pltpu.SemaphoreType.DMA((COPIES,)),
            pltpu.SemaphoreType.DMA((COPIES,)),
        ],
        compiler_params=pltpu.CompilerParams(
            collective_id=0, has_side_effects=True, vmem_limit_bytes=60 * 1024 * 1024
        ),
    )
    return kern(*operands)


def solution(mesh):
    return jax.shard_map(
        on_device,
        mesh=mesh,
        in_specs=(
            P("blk", ("grp", "wide")),
            P("blk", ("grp", "wide")),
            P(("grp", "wide"), None),
            P(("grp", "wide"), None),
            P(),
            P(),
            P(("grp", "wide", "blk"), None),
        ),
        out_specs=P(None, ("grp", "wide", "blk")),
        check_vma=False,
    )
```

```python
import functools

import jax
import jax.numpy as jnp
from jax import lax
from jax.experimental import pallas as pl
from jax.experimental.pallas import tpu as pltpu
from jax.sharding import PartitionSpec as P

SEQ = 32
SPAN = 8
MESH = pl.DeviceIdType.MESH
NT = (((1,), (1,)), ((), ()))
highest = lax.Precision.HIGHEST


def iota(shape, dim):
    return lax.broadcasted_iota(jnp.int32, shape, dim)


def dot32(a, b, dims=(((1,), (0,)), ((), ()))):
    return lax.dot_general(a, b, dims, precision=highest, preferred_element_type=jnp.float32)


def project(act_ref, grd_ref, win_ref, wout_ref, part, ready_grad, ready_act):
    pairs = 2 * part.shape[0]
    k_in, depth = win_ref.shape
    k_out = wout_ref.shape[0]
    ready_grad()
    grads = grd_ref[...].reshape(pairs, 2, SEQ, depth)
    wout = wout_ref[...]
    blank = jnp.zeros((k_out, depth), wout.dtype)
    low = None
    for q in range(2):
        weight = jnp.concatenate([wout, blank] if q == 0 else [blank, wout], axis=0)
        rows = grads[:, q].reshape(pairs * SEQ, depth)
        term = lax.dot_general(rows, weight, NT, preferred_element_type=jnp.float32)
        low = term if low is None else low + term
    part[:, :, 0:SEQ, :] = low.reshape(pairs // 2, 2, SEQ, 128)
    ready_act()
    acts = act_ref[...].reshape(pairs, 4, SEQ // 2, depth)
    win = win_ref[...]
    blank = jnp.zeros((k_in, depth), win.dtype)
    low = None
    for q in range(4):
        weight = jnp.concatenate([win if j == q else blank for j in range(4)], axis=0)
        rows = acts[:, q].reshape(pairs * SEQ // 2, depth)
        term = lax.dot_general(rows, weight, NT, preferred_element_type=jnp.float32)
        low = term if low is None else low + term
    part[:, :, SEQ:, :] = low.reshape(pairs // 2, 2, SEQ // 2, 128)


def factors(in_inverse, out_inverse):
    k_in, k_out = in_inverse.shape[0], out_inverse.shape[0]
    row, col = iota((128, k_out), 0), iota((128, k_out), 1)
    pick = jnp.where(col == 4 * ((row % 32) // 2) + row // 32, 1.0, 0.0).astype(jnp.float32)
    picked = dot32(pick, out_inverse)
    wide = jnp.concatenate([picked, picked], axis=1)
    row, col = iota((128, 128), 0), iota((128, 128), 1)
    left = jnp.where(col // k_out == row % 2, wide, 0.0)
    tall = jnp.concatenate([in_inverse] * 4, axis=0)
    right = jnp.concatenate([tall] * 4, axis=1)
    return left, right


def shape_queries(low, left, right):
    lo, li = low[:SEQ], low[SEQ:]
    first = dot32(lo[: SEQ // 2], li, (((0,), (0,)), ((), ())))
    second = dot32(lo[SEQ // 2 :], li, (((0,), (0,)), ((), ())))
    row, col = iota((128, 128), 0) // 64, iota((128, 128), 1) // 32
    gradient = jnp.where(col == 2 * row, first, jnp.where(col == 2 * row + 1, second, 0.0))
    both = dot32(left, dot32(gradient, right))
    lane = iota((32, 128), 1) // 32
    out = both[0:32]
    for k in range(1, 4):
        out = jnp.where(lane == k, both[32 * k : 32 * k + 32], out)
    return out


def influence_kernel(
    act_hbm, grd_hbm, win_hbm, wout_hbm, in_inv_hbm, out_inv_hbm, store_hbm,
    out_ref,
    act_ref, grd_ref, win_ref, wout_ref, in_inv_ref, out_inv_ref, store,
    part, from_core, half, from_group, mine, queries,
    load_sem, send_sem, recv_sem,
):
    loads = [
        pltpu.make_async_copy(src, dst, load_sem.at[n])
        for n, (src, dst) in enumerate((
            (wout_hbm, wout_ref), (grd_hbm, grd_ref), (win_hbm, win_ref), (act_hbm, act_ref),
            (in_inv_hbm, in_inv_ref), (out_inv_hbm, out_inv_ref),
        ))
    ]
    for one in loads:
        one.start()

    y = lax.axis_index("grp")
    w = lax.axis_index("wide")
    b = lax.axis_index("blk")
    ny, nz = 4, 8
    xh, c = w // 2, w % 2
    z, xl = b // 2, b % 2
    x = 2 * xh + xl
    oc = 1 - c

    def device(y_, x_, z_, c_):
        return (y_, 2 * (x_ // 2) + c_, 2 * z_ + x_ % 2)

    group = [(dy, dx) for dy in range(ny) for dx in (0, 2) if (dy, dx) != (0, 0)]
    partner = device(y, x, z, oc)
    to_group = [device((y + dy) % ny, (x + dx) % 4, z, c) for dy, dx in group]
    to_z = [device(y, x, (z + d) % nz, c) for d in range(1, nz)]
    to_x = [device(y, (x + d) % 4, z, c) for d in range(1, 4)]
    to_y = [device((y + d) % ny, x, z, c) for d in range(1, ny)]

    barrier = pltpu.get_barrier_semaphore()
    greeted = [partner] + to_group + to_z + [to_x[0], to_x[2]]
    for peer in greeted:
        pl.semaphore_signal(barrier, inc=1, device_id=peer, device_id_type=MESH)

    def arrived(first, stop):
        for one in loads[first:stop]:
            one.wait()

    project(
        act_ref, grd_ref, win_ref, wout_ref, part, lambda: arrived(0, 2), lambda: arrived(2, 4)
    )
    arrived(4, 6)
    load_store = pltpu.make_async_copy(store_hbm, store, load_sem.at[len(loads)])
    load_store.start()

    pl.semaphore_wait(barrier, len(greeted))

    used = []

    def copy(src, dst, peer):
        n = len(used)
        used.append(
            pltpu.make_async_remote_copy(
                src_ref=src, dst_ref=dst, send_sem=send_sem.at[n], recv_sem=recv_sem.at[n],
                device_id=peer, device_id_type=MESH,
            )
        )
        return used[-1]

    core = copy(part.at[:, oc], from_core, partner)
    core.start()
    left, right = factors(in_inv_ref[...], out_inv_ref[...])
    core.wait_recv()
    half[...] = part[:, c] + from_core[...]

    sums = []
    for n, (dy, dx) in enumerate(group):
        target = ((y + dy) % ny) * 2 + ((x + dx) % 4) // 2
        sums.append(copy(half.at[target], from_group.at[n], to_group[n]))
        sums[-1].start()
    low = half[y * 2 + xh]
    for n, one in enumerate(sums):
        one.wait_recv()
        low = low + from_group[n]

    rows = shape_queries(low, left, right).astype(jnp.bfloat16)
    for j in range(16):
        mine[j] = rows[2 * j : 2 * j + 2]

    base, other = 8 * c, 8 * oc
    own = pl.ds(base, 8)
    swap = copy(mine.at[pl.ds(other, 8)], queries.at[pl.ds(other, 8), z, xl, y, xh, c], partner)
    swap.start()
    queries[own, z, xl, y, xh, c] = mine[own]
    swap.wait_recv()

    def send(view, peers):
        sent = [copy(view, view, peer) for peer in peers]
        for one in sent:
            one.start()
        return sent

    def arrive(sent):
        for one in sent:
            one.wait_recv()

    def line(s, x_, y_):
        return (
            queries.at[base + 2 * s, :, x_ % 2, y, x_ // 2],
            queries.at[base + 2 * s + 1, :, xl, y_, xh],
        )

    def plane(s, x_, y_):
        return (
            queries.at[base + 2 * s, :, :, y_],
            queries.at[base + 2 * s + 1, :, x_ % 2, :, x_ // 2],
        )

    CHUNKS = 4
    columns = [send(queries.at[pl.ds(base, 2), z, xl, y, xh], to_z)]
    columns.append(send(queries.at[pl.ds(base + 2, 6), z, xl, y, xh], to_z))
    lines = []
    for s in range(CHUNKS):
        if s < 2:
            arrive(columns[s])
        along_x, along_y = line(s, x, y)
        lines.append(send(along_x, to_x) + send(along_y, to_y))
    planes = []
    for s in range(CHUNKS):
        arrive(lines[s])
        along_y, along_x = plane(s, x, y)
        planes.append(
            send(along_y, to_y) + send(along_x, to_x)
        )
    view = queries.reshape(16, 512, 128)

    def add_product(slab, first):
        rows = jnp.concatenate([view[slab + j] for j in range(SPAN)], axis=1)
        column = pl.ds(pl.multiple_of(slab * 128, 256), SPAN * 128)

        def tile(n, _):
            part_rows = pl.ds(pl.multiple_of(n * 256, 256), 256)
            term = lax.dot_general(
                rows, store[part_rows, column], NT, preferred_element_type=jnp.float32
            )
            if first:
                out_ref[:, part_rows] = term
            else:
                out_ref[:, part_rows] += term
            return 0

        lax.fori_loop(0, store.shape[0] // 256, tile, 0)

    load_store.wait()
    swaps = []
    for s in range(CHUNKS):
        arrive(planes[s])
        swaps.append(send(queries.at[pl.ds(base + 2 * s, 2)], [partner]))
        if (2 * s + 2) % SPAN == 0:
            add_product(base + 2 * s + 2 - SPAN, 2 * s + 2 == SPAN)
    for s in range(CHUNKS):
        arrive(swaps[s])
        if (2 * s + 2) % SPAN == 0:
            add_product(other + 2 * s + 2 - SPAN, False)
    for one in used:
        one.wait_send()


COPIES = 1 + 7 + 1 + 2 * 7 + 4 * (6 + 4 + 2 + 1)


def on_device(
    activations, out_grads, in_projection, out_projection, in_inverse, out_inverse, grad_store
):
    pairs = activations.shape[0] // (2 * SEQ)
    operands = (
        activations, out_grads, in_projection.T, out_projection.T, in_inverse, out_inverse,
        grad_store,
    )
    kern = pl.pallas_call(
        influence_kernel,
        out_shape=jax.ShapeDtypeStruct((512, grad_store.shape[0]), jnp.float32),
        in_specs=[pl.BlockSpec(memory_space=pltpu.HBM)] * len(operands),
        out_specs=pl.BlockSpec(memory_space=pltpu.VMEM),
        scratch_shapes=[
            *[pltpu.VMEM(one.shape, one.dtype) for one in operands],
            pltpu.VMEM((pairs // 2, 2, 48, 128), jnp.float32),
            pltpu.VMEM((pairs // 2, 48, 128), jnp.float32),
            pltpu.VMEM((pairs // 2, 48, 128), jnp.float32),
            pltpu.VMEM((7, 48, 128), jnp.float32),
            pltpu.VMEM((16, 2, 128), jnp.bfloat16),
            pltpu.VMEM((16, 8, 2, 4, 2, 2, 2, 128), jnp.bfloat16),
            pltpu.SemaphoreType.DMA((len(operands),)),
            pltpu.SemaphoreType.DMA((COPIES,)),
            pltpu.SemaphoreType.DMA((COPIES,)),
        ],
        compiler_params=pltpu.CompilerParams(
            collective_id=0, has_side_effects=True, vmem_limit_bytes=32 * 1024 * 1024
        ),
    )
    return kern(*[pltpu.with_memory_space_constraint(one, pltpu.HBM) for one in operands])


def solution(mesh):
    return jax.shard_map(
        on_device,
        mesh=mesh,
        in_specs=(
            P("blk", ("grp", "wide")),
            P("blk", ("grp", "wide")),
            P(("grp", "wide"), None),
            P(("grp", "wide"), None),
            P(),
            P(),
            P(("grp", "wide", "blk"), None),
        ),
        out_specs=P(None, ("grp", "wide", "blk")),
        check_vma=False,
    )
```

```python
import functools

import jax
import jax.numpy as jnp
from jax import lax
from jax.experimental import pallas as pl
from jax.experimental.pallas import tpu as pltpu
from jax.sharding import PartitionSpec as P

SEQ = 32
SPAN = 4
MESH = pl.DeviceIdType.MESH
NT = (((1,), (1,)), ((), ()))
highest = lax.Precision.HIGHEST


def iota(shape, dim):
    return lax.broadcasted_iota(jnp.int32, shape, dim)


def dot32(a, b, dims=(((1,), (0,)), ((), ()))):
    return lax.dot_general(a, b, dims, precision=highest, preferred_element_type=jnp.float32)


def project(act_ref, grd_ref, win_ref, wout_ref, part, ready_grad, ready_act):
    pairs = 2 * part.shape[0]
    k_in, depth = win_ref.shape
    k_out = wout_ref.shape[0]
    ready_grad()
    grads = grd_ref[...].reshape(pairs, 2, SEQ, depth)
    wout = wout_ref[...]
    blank = jnp.zeros((k_out, depth), wout.dtype)
    low = None
    for q in range(2):
        weight = jnp.concatenate([wout, blank] if q == 0 else [blank, wout], axis=0)
        rows = grads[:, q].reshape(pairs * SEQ, depth)
        term = lax.dot_general(rows, weight, NT, preferred_element_type=jnp.float32)
        low = term if low is None else low + term
    part[:, :, 0:SEQ, :] = low.reshape(pairs // 2, 2, SEQ, 128)
    ready_act()
    acts = act_ref[...].reshape(pairs, 4, SEQ // 2, depth)
    win = win_ref[...]
    blank = jnp.zeros((k_in, depth), win.dtype)
    low = None
    for q in range(4):
        weight = jnp.concatenate([win if j == q else blank for j in range(4)], axis=0)
        rows = acts[:, q].reshape(pairs * SEQ // 2, depth)
        term = lax.dot_general(rows, weight, NT, preferred_element_type=jnp.float32)
        low = term if low is None else low + term
    part[:, :, SEQ:, :] = low.reshape(pairs // 2, 2, SEQ // 2, 128)


def factors(in_inverse, out_inverse):
    k_in, k_out = in_inverse.shape[0], out_inverse.shape[0]
    row, col = iota((128, k_out), 0), iota((128, k_out), 1)
    pick = jnp.where(col == 4 * ((row % 32) // 2) + row // 32, 1.0, 0.0).astype(jnp.float32)
    picked = dot32(pick, out_inverse)
    wide = jnp.concatenate([picked, picked], axis=1)
    row, col = iota((128, 128), 0), iota((128, 128), 1)
    left = jnp.where(col // k_out == row % 2, wide, 0.0)
    tall = jnp.concatenate([in_inverse] * 4, axis=0)
    right = jnp.concatenate([tall] * 4, axis=1)
    return left, right


def shape_queries(low, left, right):
    lo, li = low[:SEQ], low[SEQ:]
    first = dot32(lo[: SEQ // 2], li, (((0,), (0,)), ((), ())))
    second = dot32(lo[SEQ // 2 :], li, (((0,), (0,)), ((), ())))
    row, col = iota((128, 128), 0) // 64, iota((128, 128), 1) // 32
    gradient = jnp.where(col == 2 * row, first, jnp.where(col == 2 * row + 1, second, 0.0))
    both = dot32(left, dot32(gradient, right))
    lane = iota((32, 128), 1) // 32
    out = both[0:32]
    for k in range(1, 4):
        out = jnp.where(lane == k, both[32 * k : 32 * k + 32], out)
    return out


def influence_kernel(
    act_hbm, grd_hbm, win_hbm, wout_hbm, in_inv_hbm, out_inv_hbm, store_hbm,
    out_ref,
    act_ref, grd_ref, win_ref, wout_ref, in_inv_ref, out_inv_ref, store,
    part, from_core, half, from_group, mine, queries, level,
    load_sem, send_sem, recv_sem,
):
    loads = [
        pltpu.make_async_copy(src, dst, load_sem.at[n])
        for n, (src, dst) in enumerate((
            (wout_hbm, wout_ref), (grd_hbm, grd_ref), (win_hbm, win_ref), (act_hbm, act_ref),
            (in_inv_hbm, in_inv_ref), (out_inv_hbm, out_inv_ref),
        ))
    ]
    for one in loads:
        one.start()

    y = lax.axis_index("grp")
    w = lax.axis_index("wide")
    b = lax.axis_index("blk")
    ny, nz = 4, 8
    xh, c = w // 2, w % 2
    z, xl = b // 2, b % 2
    x = 2 * xh + xl
    oc = 1 - c

    def device(y_, x_, z_, c_):
        return (y_, 2 * (x_ // 2) + c_, 2 * z_ + x_ % 2)

    group = [(dy, dx) for dy in range(ny) for dx in (0, 2) if (dy, dx) != (0, 0)]
    partner = device(y, x, z, oc)
    to_group = [device((y + dy) % ny, (x + dx) % 4, z, c) for dy, dx in group]
    to_z = [device(y, x, (z + d) % nz, c) for d in range(1, nz)]
    to_x = [device(y, (x + d) % 4, z, c) for d in range(1, 4)]
    to_y = [device((y + d) % ny, x, z, c) for d in range(1, ny)]

    barrier = pltpu.get_barrier_semaphore()
    greeted = [partner] + to_group + to_z + [to_x[0], to_x[2]]
    for peer in greeted:
        pl.semaphore_signal(barrier, inc=1, device_id=peer, device_id_type=MESH)

    def arrived(first, stop):
        for one in loads[first:stop]:
            one.wait()

    project(
        act_ref, grd_ref, win_ref, wout_ref, part, lambda: arrived(0, 2), lambda: arrived(2, 4)
    )
    arrived(4, 6)
    load_store = pltpu.make_async_copy(store_hbm, store, load_sem.at[len(loads)])
    load_store.start()

    pl.semaphore_wait(barrier, len(greeted))

    used = []

    def copy(src, dst, peer):
        n = len(used)
        used.append(
            pltpu.make_async_remote_copy(
                src_ref=src, dst_ref=dst, send_sem=send_sem.at[n], recv_sem=recv_sem.at[n],
                device_id=peer, device_id_type=MESH,
            )
        )
        return used[-1]

    core = copy(part.at[:, oc], from_core, partner)
    core.start()
    left, right = factors(in_inv_ref[...], out_inv_ref[...])
    core.wait_recv()
    half[...] = part[:, c] + from_core[...]

    sums = []
    for n, (dy, dx) in enumerate(group):
        target = ((y + dy) % ny) * 2 + ((x + dx) % 4) // 2
        sums.append(copy(half.at[target], from_group.at[n], to_group[n]))
        sums[-1].start()
    low = half[y * 2 + xh]
    for n, one in enumerate(sums):
        one.wait_recv()
        low = low + from_group[n]

    rows = shape_queries(low, left, right).astype(jnp.bfloat16)
    for j in range(16):
        mine[j] = rows[2 * j : 2 * j + 2]

    base, other = 8 * c, 8 * oc
    own = pl.ds(base, 8)
    swap = copy(mine.at[pl.ds(other, 8)], queries.at[pl.ds(other, 8), z, xl, y, xh, c], partner)
    swap.start()
    queries[own, z, xl, y, xh, c] = mine[own]
    swap.wait_recv()

    def send(view, peers):
        sent = [copy(view, view, peer) for peer in peers]
        for one in sent:
            one.start()
        return sent

    def arrive(sent):
        for one in sent:
            one.wait_recv()

    left_already = set()

    def leave(sent):
        for one in sent:
            one.wait_send()
        left_already.update(id(one) for one in sent)

    def split(h):
        return pl.ds(base + 4 * h, 2), pl.ds(base + 4 * h + 2, 2)

    def start_columns(h):
        return send(queries.at[pl.ds(base + 4 * h, 4), z, xl, y, xh], to_z)

    def start_lines(h):
        first, second = split(h)
        return send(queries.at[first, :, xl, y, xh], to_x) + send(
            queries.at[second, :, xl, y, xh], to_y
        )

    def start_planes(h):
        first, second = split(h)
        return send(queries.at[first, :, :, y], to_y) + send(
            queries.at[second, :, xl, :, xh], to_x
        )

    view = queries.reshape(16, 512, 128)

    def start_swap(h):
        span = pl.ds(base + 4 * h, 4)
        one = copy(view.at[span], level.at[span], partner)
        one.start()
        return [one]

    columns = [start_columns(0), start_columns(1)]
    arrive(columns[0])
    lines = [start_lines(0)]
    arrive(columns[1])
    lines.append(start_lines(1))
    arrive(lines[0])
    planes = [start_planes(0)]
    arrive(lines[1])

    def add_product(source, slab, first):
        rows = jnp.concatenate([source[slab + j] for j in range(SPAN)], axis=1)
        column = pl.ds(pl.multiple_of(slab * 128, 256), SPAN * 128)

        def tile(n, _):
            part_rows = pl.ds(pl.multiple_of(n * 256, 256), 256)
            term = lax.dot_general(
                rows, store[part_rows, column], NT, preferred_element_type=jnp.float32
            )
            if first:
                out_ref[:, part_rows] = term
            else:
                out_ref[:, part_rows] += term
            return 0

        lax.fori_loop(0, store.shape[0] // 256, tile, 0, unroll=6)

    load_store.wait()
    planes.append(start_planes(1))
    arrive(planes[0])
    swaps = [start_swap(0)]
    add_product(view, base, True)
    arrive(swaps[0])
    add_product(level, other, False)
    arrive(planes[1])
    swaps.append(start_swap(1))
    add_product(view, base + 4, False)
    arrive(swaps[1])
    add_product(level, other + 4, False)
    for one in used:
        if id(one) not in left_already:
            one.wait_send()


COPIES = 1 + 7 + 1 + 2 * (7 + 6 + 6 + 1)


def on_device(
    activations, out_grads, in_projection, out_projection, in_inverse, out_inverse, grad_store
):
    pairs = activations.shape[0] // (2 * SEQ)
    operands = (
        activations, out_grads, in_projection.T, out_projection.T, in_inverse, out_inverse,
        grad_store,
    )
    kern = pl.pallas_call(
        influence_kernel,
        out_shape=jax.ShapeDtypeStruct((512, grad_store.shape[0]), jnp.float32),
        in_specs=[pl.BlockSpec(memory_space=pltpu.HBM)] * len(operands),
        out_specs=pl.BlockSpec(memory_space=pltpu.VMEM),
        scratch_shapes=[
            *[pltpu.VMEM(one.shape, one.dtype) for one in operands],
            pltpu.VMEM((pairs // 2, 2, 48, 128), jnp.float32),
            pltpu.VMEM((pairs // 2, 48, 128), jnp.float32),
            pltpu.VMEM((pairs // 2, 48, 128), jnp.float32),
            pltpu.VMEM((7, 48, 128), jnp.float32),
            pltpu.VMEM((16, 2, 128), jnp.bfloat16),
            pltpu.VMEM((16, 8, 2, 4, 2, 2, 2, 128), jnp.bfloat16),
            pltpu.VMEM((16, 512, 128), jnp.bfloat16),
            pltpu.SemaphoreType.DMA((len(operands),)),
            pltpu.SemaphoreType.DMA((COPIES,)),
            pltpu.SemaphoreType.DMA((COPIES,)),
        ],
        compiler_params=pltpu.CompilerParams(
            collective_id=0, has_side_effects=True, vmem_limit_bytes=32 * 1024 * 1024
        ),
    )
    return kern(*[pltpu.with_memory_space_constraint(one, pltpu.HBM) for one in operands])


def solution(mesh):
    return jax.shard_map(
        on_device,
        mesh=mesh,
        in_specs=(
            P("blk", ("grp", "wide")),
            P("blk", ("grp", "wide")),
            P(("grp", "wide"), None),
            P(("grp", "wide"), None),
            P(),
            P(),
            P(("grp", "wide", "blk"), None),
        ),
        out_specs=P(None, ("grp", "wide", "blk")),
        check_vma=False,
    )
```

```python
import functools

import jax
import jax.numpy as jnp
from jax import lax
from jax.experimental import pallas as pl
from jax.experimental.pallas import tpu as pltpu
from jax.sharding import PartitionSpec as P

SEQ = 32
SPAN = 8
MESH = pl.DeviceIdType.MESH
NT = (((1,), (1,)), ((), ()))
highest = lax.Precision.HIGHEST


def iota(shape, dim):
    return lax.broadcasted_iota(jnp.int32, shape, dim)


def dot32(a, b, dims=(((1,), (0,)), ((), ()))):
    return lax.dot_general(a, b, dims, precision=highest, preferred_element_type=jnp.float32)


def project(act_ref, grd_ref, win_ref, wout_ref, part, ready_grad, ready_act):
    pairs = 2 * part.shape[0]
    k_in, depth = win_ref.shape
    k_out = wout_ref.shape[0]
    ready_grad()
    grads = grd_ref[...].reshape(pairs, 2, SEQ, depth)
    wout = wout_ref[...]
    blank = jnp.zeros((k_out, depth), wout.dtype)
    low = None
    for q in range(2):
        weight = jnp.concatenate([wout, blank] if q == 0 else [blank, wout], axis=0)
        rows = grads[:, q].reshape(pairs * SEQ, depth)
        term = lax.dot_general(rows, weight, NT, preferred_element_type=jnp.float32)
        low = term if low is None else low + term
    part[:, :, 0:SEQ, :] = low.reshape(pairs // 2, 2, SEQ, 128)
    ready_act()
    acts = act_ref[...].reshape(pairs, 4, SEQ // 2, depth)
    win = win_ref[...]
    blank = jnp.zeros((k_in, depth), win.dtype)
    low = None
    for q in range(4):
        weight = jnp.concatenate([win if j == q else blank for j in range(4)], axis=0)
        rows = acts[:, q].reshape(pairs * SEQ // 2, depth)
        term = lax.dot_general(rows, weight, NT, preferred_element_type=jnp.float32)
        low = term if low is None else low + term
    part[:, :, SEQ:, :] = low.reshape(pairs // 2, 2, SEQ // 2, 128)


def factors(in_inverse, out_inverse):
    k_in, k_out = in_inverse.shape[0], out_inverse.shape[0]
    row, col = iota((128, k_out), 0), iota((128, k_out), 1)
    pick = jnp.where(col == 4 * ((row % 32) // 2) + row // 32, 1.0, 0.0).astype(jnp.float32)
    picked = dot32(pick, out_inverse)
    wide = jnp.concatenate([picked, picked], axis=1)
    row, col = iota((128, 128), 0), iota((128, 128), 1)
    left = jnp.where(col // k_out == row % 2, wide, 0.0)
    tall = jnp.concatenate([in_inverse] * 4, axis=0)
    right = jnp.concatenate([tall] * 4, axis=1)
    return left, right


def shape_queries(low, left, right):
    lo, li = low[:SEQ], low[SEQ:]
    first = dot32(lo[: SEQ // 2], li, (((0,), (0,)), ((), ())))
    second = dot32(lo[SEQ // 2 :], li, (((0,), (0,)), ((), ())))
    row, col = iota((128, 128), 0) // 64, iota((128, 128), 1) // 32
    gradient = jnp.where(col == 2 * row, first, jnp.where(col == 2 * row + 1, second, 0.0))
    both = dot32(left, dot32(gradient, right))
    lane = iota((32, 128), 1) // 32
    out = both[0:32]
    for k in range(1, 4):
        out = jnp.where(lane == k, both[32 * k : 32 * k + 32], out)
    return out


def influence_kernel(
    act_hbm, grd_hbm, win_hbm, wout_hbm, in_inv_hbm, out_inv_hbm, store_hbm,
    out_ref,
    act_ref, grd_ref, win_ref, wout_ref, in_inv_ref, out_inv_ref, store,
    part, from_core, half, from_group, mine, queries, level,
    load_sem, send_sem, recv_sem,
):
    loads = [
        pltpu.make_async_copy(src, dst, load_sem.at[n])
        for n, (src, dst) in enumerate((
            (wout_hbm, wout_ref), (grd_hbm, grd_ref), (win_hbm, win_ref), (act_hbm, act_ref),
            (in_inv_hbm, in_inv_ref), (out_inv_hbm, out_inv_ref),
        ))
    ]
    for one in loads:
        one.start()

    y = lax.axis_index("grp")
    w = lax.axis_index("wide")
    b = lax.axis_index("blk")
    ny, nz = 4, 8
    xh, c = w // 2, w % 2
    z, xl = b // 2, b % 2
    x = 2 * xh + xl
    oc = 1 - c

    def device(y_, x_, z_, c_):
        return (y_, 2 * (x_ // 2) + c_, 2 * z_ + x_ % 2)

    group = [(2, 2), (1, 2), (3, 2), (2, 0), (0, 2), (1, 0), (3, 0)]
    partner = device(y, x, z, oc)
    to_group = [device((y + dy) % ny, (x + dx) % 4, z, c) for dy, dx in group]
    to_z = [device(y, x, (z + d) % nz, c) for d in range(1, nz)]
    to_x = [device(y, (x + d) % 4, z, c) for d in range(1, 4)]
    to_y = [device((y + d) % ny, x, z, c) for d in range(1, ny)]

    barrier = pltpu.get_barrier_semaphore()
    greeted = [partner] + to_group + to_z + [to_x[0], to_x[2]]
    for peer in greeted:
        pl.semaphore_signal(barrier, inc=1, device_id=peer, device_id_type=MESH)

    def arrived(first, stop):
        for one in loads[first:stop]:
            one.wait()

    project(
        act_ref, grd_ref, win_ref, wout_ref, part, lambda: arrived(0, 2), lambda: arrived(2, 4)
    )
    arrived(4, 6)
    load_store = pltpu.make_async_copy(store_hbm, store, load_sem.at[len(loads)])
    load_store.start()

    pl.semaphore_wait(barrier, len(greeted))

    used = []

    def copy(src, dst, peer):
        n = len(used)
        used.append(
            pltpu.make_async_remote_copy(
                src_ref=src, dst_ref=dst, send_sem=send_sem.at[n], recv_sem=recv_sem.at[n],
                device_id=peer, device_id_type=MESH,
            )
        )
        return used[-1]

    core = copy(part.at[:, oc], from_core, partner)
    core.start()
    left, right = factors(in_inv_ref[...], out_inv_ref[...])
    core.wait_recv()
    half[...] = part[:, c] + from_core[...]

    sums = []
    for n, (dy, dx) in enumerate(group):
        target = ((y + dy) % ny) * 2 + ((x + dx) % 4) // 2
        sums.append(copy(half.at[target], from_group.at[n], to_group[n]))
        sums[-1].start()
    low = half[y * 2 + xh]
    for n, one in enumerate(sums):
        one.wait_recv()
        low = low + from_group[n]

    rows = shape_queries(low, left, right).astype(jnp.bfloat16)
    for j in range(16):
        mine[j] = rows[2 * j : 2 * j + 2]

    base, other = 8 * c, 8 * oc
    own = pl.ds(base, 8)
    swap = copy(mine.at[pl.ds(other, 8)], queries.at[pl.ds(other, 8), z, xl, y, xh, c], partner)
    swap.start()
    queries[own, z, xl, y, xh, c] = mine[own]
    swap.wait_recv()

    def send(view, peers):
        sent = [copy(view, view, peer) for peer in peers]
        for one in sent:
            one.start()
        return sent

    def arrive(sent):
        for one in sent:
            one.wait_recv()

    view = queries.reshape(16, 512, 128)
    first, second = pl.ds(base, 4), pl.ds(base + 4, 4)
    far_x, far_y = [to_x[1], to_x[0], to_x[2]], [to_y[1], to_y[0], to_y[2]]

    def start_lines(z_):
        return send(queries.at[first, z_, xl, y, xh], far_x) + send(
            queries.at[second, z_, xl, y, xh], far_y
        )

    def start_planes(z_):
        return send(queries.at[first, z_, :, y], far_y) + send(
            queries.at[second, z_, xl, :, xh], far_x
        )

    def start_swap(z_):
        rows = pl.ds(pl.multiple_of(64 * z_, 64), 64)
        one = copy(view.at[own, rows], level.at[own, rows], partner)
        one.start()
        return [one]

    def block(d):
        return (z + nz - d) % nz

    columns, lines, planes, swaps = {}, {}, {}, {}
    for d in (4, 3, 5, 2, 6, 1, 7):
        columns[d] = send(queries.at[own, z, xl, y, xh], [to_z[d - 1]])
    lines[0] = start_lines(z)

    def next_line(d):
        arrive(columns[d])
        lines[d] = start_lines(block(d))

    def next_plane(d):
        arrive(lines[d])
        planes[d] = start_planes(block(d))

    for d in (1, 7, 2, 6):
        next_line(d)
    next_plane(0)
    for d in (3, 5, 4):
        next_line(d)
    for d in (1, 7, 2, 6, 3, 5, 4):
        next_plane(d)
    for d in (0, 1, 7, 2, 6, 3, 5, 4):
        arrive(planes[d])
        swaps[d] = start_swap(block(d))

    def add_product(source, slab, first):
        rows = jnp.concatenate([source[slab + j] for j in range(SPAN)], axis=1)
        column = pl.ds(pl.multiple_of(slab * 128, 256), SPAN * 128)

        def tile(n, _):
            part_rows = pl.ds(pl.multiple_of(n * 256, 256), 256)
            term = lax.dot_general(
                rows, store[part_rows, column], NT, preferred_element_type=jnp.float32
            )
            if first:
                out_ref[:, part_rows] = term
            else:
                out_ref[:, part_rows] += term
            return 0

        lax.fori_loop(0, store.shape[0] // 256, tile, 0, unroll=6)

    load_store.wait()
    add_product(view, base, True)
    for d in range(nz):
        arrive(swaps[d])
    add_product(level, other, False)
    for one in used:
        one.wait_send()


COPIES = 1 + 7 + 1 + 7 + 8 * (6 + 6 + 1)


def on_device(
    activations, out_grads, in_projection, out_projection, in_inverse, out_inverse, grad_store
):
    pairs = activations.shape[0] // (2 * SEQ)
    operands = (
        activations, out_grads, in_projection.T, out_projection.T, in_inverse, out_inverse,
        grad_store,
    )
    kern = pl.pallas_call(
        influence_kernel,
        out_shape=jax.ShapeDtypeStruct((512, grad_store.shape[0]), jnp.float32),
        in_specs=[pl.BlockSpec(memory_space=pltpu.HBM)] * len(operands),
        out_specs=pl.BlockSpec(memory_space=pltpu.VMEM),
        scratch_shapes=[
            *[pltpu.VMEM(one.shape, one.dtype) for one in operands],
            pltpu.VMEM((pairs // 2, 2, 48, 128), jnp.float32),
            pltpu.VMEM((pairs // 2, 48, 128), jnp.float32),
            pltpu.VMEM((pairs // 2, 48, 128), jnp.float32),
            pltpu.VMEM((7, 48, 128), jnp.float32),
            pltpu.VMEM((16, 2, 128), jnp.bfloat16),
            pltpu.VMEM((16, 8, 2, 4, 2, 2, 2, 128), jnp.bfloat16),
            pltpu.VMEM((16, 512, 128), jnp.bfloat16),
            pltpu.SemaphoreType.DMA((len(operands),)),
            pltpu.SemaphoreType.DMA((COPIES,)),
            pltpu.SemaphoreType.DMA((COPIES,)),
        ],
        compiler_params=pltpu.CompilerParams(
            collective_id=0, has_side_effects=True, vmem_limit_bytes=32 * 1024 * 1024
        ),
    )
    return kern(*[pltpu.with_memory_space_constraint(one, pltpu.HBM) for one in operands])


def solution(mesh):
    return jax.shard_map(
        on_device,
        mesh=mesh,
        in_specs=(
            P("blk", ("grp", "wide")),
            P("blk", ("grp", "wide")),
            P(("grp", "wide"), None),
            P(("grp", "wide"), None),
            P(),
            P(),
            P(("grp", "wide", "blk"), None),
        ),
        out_specs=P(None, ("grp", "wide", "blk")),
        check_vma=False,
    )
```

```python
import functools

import jax
import jax.numpy as jnp
from jax import lax
from jax.experimental import pallas as pl
from jax.experimental.pallas import tpu as pltpu
from jax.sharding import PartitionSpec as P

SEQ = 32
SPAN = 8
REL = (0, 1, 7, 2, 6, 3, 5, 4)
RUNS = ((0, 1), (1, 2), (3, 2), (5, 3))
MESH = pl.DeviceIdType.MESH
NT = (((1,), (1,)), ((), ()))
highest = lax.Precision.HIGHEST


def iota(shape, dim):
    return lax.broadcasted_iota(jnp.int32, shape, dim)


def dot32(a, b, dims=(((1,), (0,)), ((), ()))):
    return lax.dot_general(a, b, dims, precision=highest, preferred_element_type=jnp.float32)


def project(act_ref, grd_ref, win_ref, wout_ref, part, ready_grad, ready_act):
    pairs = 2 * part.shape[0]
    k_in, depth = win_ref.shape
    k_out = wout_ref.shape[0]
    ready_grad()
    grads = grd_ref[...].reshape(pairs, 2, SEQ, depth)
    wout = wout_ref[...]
    blank = jnp.zeros((k_out, depth), wout.dtype)
    low = None
    for q in range(2):
        weight = jnp.concatenate([wout, blank] if q == 0 else [blank, wout], axis=0)
        rows = grads[:, q].reshape(pairs * SEQ, depth)
        term = lax.dot_general(rows, weight, NT, preferred_element_type=jnp.float32)
        low = term if low is None else low + term
    part[:, :, 0:SEQ, :] = low.reshape(pairs // 2, 2, SEQ, 128)
    ready_act()
    acts = act_ref[...].reshape(pairs, 4, SEQ // 2, depth)
    win = win_ref[...]
    blank = jnp.zeros((k_in, depth), win.dtype)
    low = None
    for q in range(4):
        weight = jnp.concatenate([win if j == q else blank for j in range(4)], axis=0)
        rows = acts[:, q].reshape(pairs * SEQ // 2, depth)
        term = lax.dot_general(rows, weight, NT, preferred_element_type=jnp.float32)
        low = term if low is None else low + term
    part[:, :, SEQ:, :] = low.reshape(pairs // 2, 2, SEQ // 2, 128)


def factors(in_inverse, out_inverse):
    k_in, k_out = in_inverse.shape[0], out_inverse.shape[0]
    row, col = iota((128, k_out), 0), iota((128, k_out), 1)
    pick = jnp.where(col == 4 * ((row % 32) // 2) + row // 32, 1.0, 0.0).astype(jnp.float32)
    picked = dot32(pick, out_inverse)
    wide = jnp.concatenate([picked, picked], axis=1)
    row, col = iota((128, 128), 0), iota((128, 128), 1)
    left = jnp.where(col // k_out == row % 2, wide, 0.0)
    tall = jnp.concatenate([in_inverse] * 4, axis=0)
    right = jnp.concatenate([tall] * 4, axis=1)
    return left, right


def shape_queries(low, left, right):
    lo, li = low[:SEQ], low[SEQ:]
    first = dot32(lo[: SEQ // 2], li, (((0,), (0,)), ((), ())))
    second = dot32(lo[SEQ // 2 :], li, (((0,), (0,)), ((), ())))
    row, col = iota((128, 128), 0) // 64, iota((128, 128), 1) // 32
    gradient = jnp.where(col == 2 * row, first, jnp.where(col == 2 * row + 1, second, 0.0))
    both = dot32(left, dot32(gradient, right))
    lane = iota((32, 128), 1) // 32
    out = both[0:32]
    for k in range(1, 4):
        out = jnp.where(lane == k, both[32 * k : 32 * k + 32], out)
    return out


def influence_kernel(
    act_hbm, grd_hbm, win_hbm, wout_hbm, in_inv_hbm, out_inv_hbm, store_hbm,
    out_ref,
    act_ref, grd_ref, win_ref, wout_ref, in_inv_ref, out_inv_ref, store,
    part, from_core, half, from_group, mine, queries, level,
    load_sem, send_sem, recv_sem,
):
    loads = [
        pltpu.make_async_copy(src, dst, load_sem.at[n])
        for n, (src, dst) in enumerate((
            (wout_hbm, wout_ref), (grd_hbm, grd_ref), (win_hbm, win_ref), (act_hbm, act_ref),
            (in_inv_hbm, in_inv_ref), (out_inv_hbm, out_inv_ref),
        ))
    ]
    for one in loads:
        one.start()

    y = lax.axis_index("grp")
    w = lax.axis_index("wide")
    b = lax.axis_index("blk")
    ny, nz = 4, 8
    xh, c = w // 2, w % 2
    z, xl = b // 2, b % 2
    x = 2 * xh + xl
    oc = 1 - c

    def device(y_, x_, z_, c_):
        return (y_, 2 * (x_ // 2) + c_, 2 * z_ + x_ % 2)

    group = [(2, 2), (1, 2), (3, 2), (2, 0), (0, 2), (1, 0), (3, 0)]
    partner = device(y, x, z, oc)
    to_group = [device((y + dy) % ny, (x + dx) % 4, z, c) for dy, dx in group]
    to_z = [device(y, x, (z + d) % nz, c) for d in range(1, nz)]
    to_x = [device(y, (x + d) % 4, z, c) for d in range(1, 4)]
    to_y = [device((y + d) % ny, x, z, c) for d in range(1, ny)]

    barrier = pltpu.get_barrier_semaphore()
    greeted = [partner] + to_group + to_z + [to_x[0], to_x[2]]
    for peer in greeted:
        pl.semaphore_signal(barrier, inc=1, device_id=peer, device_id_type=MESH)

    def arrived(first, stop):
        for one in loads[first:stop]:
            one.wait()

    project(
        act_ref, grd_ref, win_ref, wout_ref, part, lambda: arrived(0, 2), lambda: arrived(2, 4)
    )
    arrived(4, 6)
    load_store = pltpu.make_async_copy(store_hbm, store, load_sem.at[len(loads)])
    load_store.start()

    pl.semaphore_wait(barrier, len(greeted))

    used = []

    def copy(src, dst, peer):
        n = len(used)
        used.append(
            pltpu.make_async_remote_copy(
                src_ref=src, dst_ref=dst, send_sem=send_sem.at[n], recv_sem=recv_sem.at[n],
                device_id=peer, device_id_type=MESH,
            )
        )
        return used[-1]

    core = copy(part.at[:, oc], from_core, partner)
    core.start()
    left, right = factors(in_inv_ref[...], out_inv_ref[...])
    core.wait_recv()
    half[...] = part[:, c] + from_core[...]

    sums = []
    for n, (dy, dx) in enumerate(group):
        target = ((y + dy) % ny) * 2 + ((x + dx) % 4) // 2
        sums.append(copy(half.at[target], from_group.at[n], to_group[n]))
        sums[-1].start()
    low = half[y * 2 + xh]
    for n, one in enumerate(sums):
        one.wait_recv()
        low = low + from_group[n]

    rows = shape_queries(low, left, right).astype(jnp.bfloat16)
    for j in range(16):
        mine[j] = rows[2 * j : 2 * j + 2]

    base, other = 8 * c, 8 * oc
    own = pl.ds(base, 8)
    swap = copy(mine.at[pl.ds(other, 8)], queries.at[pl.ds(other, 8), 0, xl, y, xh, c], partner)
    swap.start()
    queries[own, 0, xl, y, xh, c] = mine[own]
    swap.wait_recv()

    def send(view, peers):
        sent = [copy(view, view, peer) for peer in peers]
        for one in sent:
            one.start()
        return sent

    def arrive(sent):
        for one in sent:
            one.wait_recv()

    view = queries.reshape(16, 512, 128)
    first, second = pl.ds(base, 4), pl.ds(base + 4, 4)
    far_x, far_y = [to_x[1], to_x[0], to_x[2]], [to_y[1], to_y[0], to_y[2]]

    def start_lines(run):
        at = pl.ds(*run)
        return send(queries.at[first, at, xl, y, xh], far_x) + send(
            queries.at[second, at, xl, y, xh], far_y
        )

    def start_planes(run):
        at = pl.ds(*run)
        return send(queries.at[first, at, :, y], far_y) + send(
            queries.at[second, at, xl, :, xh], far_x
        )

    def start_swap(run):
        rows = pl.ds(64 * run[0], 64 * run[1])
        one = copy(view.at[own, rows], level.at[own, rows], partner)
        one.start()
        return [one]

    columns, lines, planes, swaps = {}, [], [], []
    for r in (4, 3, 5, 2, 6, 1, 7):
        columns[r] = copy(
            queries.at[own, 0, xl, y, xh],
            queries.at[own, REL.index(r), xl, y, xh],
            to_z[nz - r - 1],
        )
        columns[r].start()
    lines.append(start_lines(RUNS[0]))

    def next_line():
        run = RUNS[len(lines)]
        arrive([columns[r] for r in REL[run[0] : run[0] + run[1]]])
        lines.append(start_lines(run))

    def next_plane():
        arrive(lines[len(planes)])
        planes.append(start_planes(RUNS[len(planes)]))

    next_line()
    next_line()
    next_plane()
    next_line()
    next_plane()
    next_plane()
    next_plane()
    for n, run in enumerate(RUNS):
        arrive(planes[n])
        swaps.append(start_swap(run))

    def add_product(source, slab, first):
        rows = jnp.concatenate([source[slab + j] for j in range(SPAN)], axis=1)
        column = pl.ds(pl.multiple_of(slab * 128, 256), SPAN * 128)

        def tile(step, _):
            part_rows = pl.ds(pl.multiple_of(step * 256, 256), 256)
            term = lax.dot_general(
                rows, store[part_rows, column], NT, preferred_element_type=jnp.float32
            )
            for n, r in enumerate(REL):
                to = pl.ds(pl.multiple_of(64 * lax.rem(z + r, nz), 64), 64)
                block = term[64 * n : 64 * n + 64]
                if first:
                    out_ref[to, part_rows] = block
                else:
                    out_ref[to, part_rows] += block
            return 0

        lax.fori_loop(0, store.shape[0] // 256, tile, 0, unroll=6)

    load_store.wait()
    add_product(view, base, True)
    for one in swaps:
        arrive(one)
    add_product(level, other, False)
    for one in used:
        one.wait_send()


COPIES = 1 + 7 + 1 + 7 + len(RUNS) * (6 + 6 + 1)


def on_device(
    activations, out_grads, in_projection, out_projection, in_inverse, out_inverse, grad_store
):
    pairs = activations.shape[0] // (2 * SEQ)
    operands = (
        activations, out_grads, in_projection.T, out_projection.T, in_inverse, out_inverse,
        grad_store,
    )
    kern = pl.pallas_call(
        influence_kernel,
        out_shape=jax.ShapeDtypeStruct((512, grad_store.shape[0]), jnp.float32),
        in_specs=[pl.BlockSpec(memory_space=pltpu.HBM)] * len(operands),
        out_specs=pl.BlockSpec(memory_space=pltpu.VMEM),
        scratch_shapes=[
            *[pltpu.VMEM(one.shape, one.dtype) for one in operands],
            pltpu.VMEM((pairs // 2, 2, 48, 128), jnp.float32),
            pltpu.VMEM((pairs // 2, 48, 128), jnp.float32),
            pltpu.VMEM((pairs // 2, 48, 128), jnp.float32),
            pltpu.VMEM((7, 48, 128), jnp.float32),
            pltpu.VMEM((16, 2, 128), jnp.bfloat16),
            pltpu.VMEM((16, 8, 2, 4, 2, 2, 2, 128), jnp.bfloat16),
            pltpu.VMEM((16, 512, 128), jnp.bfloat16),
            pltpu.SemaphoreType.DMA((len(operands),)),
            pltpu.SemaphoreType.DMA((COPIES,)),
            pltpu.SemaphoreType.DMA((COPIES,)),
        ],
        compiler_params=pltpu.CompilerParams(
            collective_id=0, has_side_effects=True, vmem_limit_bytes=32 * 1024 * 1024
        ),
    )
    return kern(*[pltpu.with_memory_space_constraint(one, pltpu.HBM) for one in operands])


def solution(mesh):
    return jax.shard_map(
        on_device,
        mesh=mesh,
        in_specs=(
            P("blk", ("grp", "wide")),
            P("blk", ("grp", "wide")),
            P(("grp", "wide"), None),
            P(("grp", "wide"), None),
            P(),
            P(),
            P(("grp", "wide", "blk"), None),
        ),
        out_specs=P(None, ("grp", "wide", "blk")),
        check_vma=False,
    )
```

```python
import functools

import jax
import jax.numpy as jnp
from jax import lax
from jax.experimental import pallas as pl
from jax.experimental.pallas import tpu as pltpu
from jax.sharding import PartitionSpec as P

SEQ = 32
SPAN = 8
REL = (0, 1, 7, 2, 6, 3, 5, 4)
RUNS = ((0, 1), (1, 2), (3, 2), (5, 3))
MESH = pl.DeviceIdType.MESH
NT = (((1,), (1,)), ((), ()))
highest = lax.Precision.HIGHEST


def iota(shape, dim):
    return lax.broadcasted_iota(jnp.int32, shape, dim)


def dot32(a, b, dims=(((1,), (0,)), ((), ()))):
    return lax.dot_general(a, b, dims, precision=highest, preferred_element_type=jnp.float32)


def project(act_ref, grd_ref, win_ref, wout_ref, part, ready_grad, ready_act):
    pairs = 2 * part.shape[0]
    k_in, depth = win_ref.shape
    k_out = wout_ref.shape[0]
    ready_grad()
    grads = grd_ref[...].reshape(pairs, 2, SEQ, depth)
    wout = wout_ref[...]
    blank = jnp.zeros((k_out, depth), wout.dtype)
    low = None
    for q in range(2):
        weight = jnp.concatenate([wout, blank] if q == 0 else [blank, wout], axis=0)
        rows = grads[:, q].reshape(pairs * SEQ, depth)
        term = lax.dot_general(rows, weight, NT, preferred_element_type=jnp.float32)
        low = term if low is None else low + term
    part[:, :, 0:SEQ, :] = low.reshape(pairs // 2, 2, SEQ, 128)
    ready_act()
    acts = act_ref[...].reshape(pairs, 4, SEQ // 2, depth)
    win = win_ref[...]
    blank = jnp.zeros((k_in, depth), win.dtype)
    low = None
    for q in range(4):
        weight = jnp.concatenate([win if j == q else blank for j in range(4)], axis=0)
        rows = acts[:, q].reshape(pairs * SEQ // 2, depth)
        term = lax.dot_general(rows, weight, NT, preferred_element_type=jnp.float32)
        low = term if low is None else low + term
    part[:, :, SEQ:, :] = low.reshape(pairs // 2, 2, SEQ // 2, 128)


def factors(in_inverse, out_inverse):
    k_in, k_out = in_inverse.shape[0], out_inverse.shape[0]
    row, col = iota((128, k_out), 0), iota((128, k_out), 1)
    pick = jnp.where(col == 4 * ((row % 32) // 2) + row // 32, 1.0, 0.0).astype(jnp.float32)
    picked = dot32(pick, out_inverse)
    wide = jnp.concatenate([picked, picked], axis=1)
    row, col = iota((128, 128), 0), iota((128, 128), 1)
    left = jnp.where(col // k_out == row % 2, wide, 0.0)
    tall = jnp.concatenate([in_inverse] * 4, axis=0)
    right = jnp.concatenate([tall] * 4, axis=1)
    return left, right


def shape_queries(low, left, right):
    lo, li = low[:SEQ], low[SEQ:]
    first = dot32(lo[: SEQ // 2], li, (((0,), (0,)), ((), ())))
    second = dot32(lo[SEQ // 2 :], li, (((0,), (0,)), ((), ())))
    row, col = iota((128, 128), 0) // 64, iota((128, 128), 1) // 32
    gradient = jnp.where(col == 2 * row, first, jnp.where(col == 2 * row + 1, second, 0.0))
    both = dot32(left, dot32(gradient, right))
    lane = iota((32, 128), 1) // 32
    out = both[0:32]
    for k in range(1, 4):
        out = jnp.where(lane == k, both[32 * k : 32 * k + 32], out)
    return out


def influence_kernel(
    act_hbm, grd_hbm, win_hbm, wout_hbm, in_inv_hbm, out_inv_hbm, store_hbm,
    out_ref,
    act_ref, grd_ref, win_ref, wout_ref, in_inv_ref, out_inv_ref, store,
    part, from_core, half, from_group, mine, theirs, queries, level,
    load_sem, send_sem, recv_sem,
):
    loads = [
        pltpu.make_async_copy(src, dst, load_sem.at[n])
        for n, (src, dst) in enumerate((
            (wout_hbm, wout_ref), (grd_hbm, grd_ref), (win_hbm, win_ref), (act_hbm, act_ref),
            (in_inv_hbm, in_inv_ref), (out_inv_hbm, out_inv_ref),
        ))
    ]
    for one in loads:
        one.start()

    y = lax.axis_index("grp")
    w = lax.axis_index("wide")
    b = lax.axis_index("blk")
    ny, nz = 4, 8
    xh, c = w // 2, w % 2
    z, xl = b // 2, b % 2
    x = 2 * xh + xl
    oc = 1 - c

    def device(y_, x_, z_, c_):
        return (y_, 2 * (x_ // 2) + c_, 2 * z_ + x_ % 2)

    group = [(2, 2), (1, 2), (3, 2), (2, 0), (0, 2), (1, 0), (3, 0)]
    partner = device(y, x, z, oc)
    to_group = [device((y + dy) % ny, (x + dx) % 4, z, c) for dy, dx in group]
    to_z = [device(y, x, (z + d) % nz, c) for d in range(1, nz)]
    to_x = [device(y, (x + d) % 4, z, c) for d in range(1, 4)]
    to_y = [device((y + d) % ny, x, z, c) for d in range(1, ny)]

    barrier = pltpu.get_barrier_semaphore()
    greeted = [partner] + to_group + to_z + [to_x[0], to_x[2]]
    for peer in greeted:
        pl.semaphore_signal(barrier, inc=1, device_id=peer, device_id_type=MESH)

    def arrived(first, stop):
        for one in loads[first:stop]:
            one.wait()

    project(
        act_ref, grd_ref, win_ref, wout_ref, part, lambda: arrived(0, 2), lambda: arrived(2, 4)
    )
    arrived(4, 6)
    load_store = pltpu.make_async_copy(store_hbm, store, load_sem.at[len(loads)])
    load_store.start()

    pl.semaphore_wait(barrier, len(greeted))

    used = []

    def copy(src, dst, peer):
        n = len(used)
        used.append(
            pltpu.make_async_remote_copy(
                src_ref=src, dst_ref=dst, send_sem=send_sem.at[n], recv_sem=recv_sem.at[n],
                device_id=peer, device_id_type=MESH,
            )
        )
        return used[-1]

    core = copy(part.at[:, oc], from_core, partner)
    core.start()
    left, right = factors(in_inv_ref[...], out_inv_ref[...])
    core.wait_recv()
    half[...] = part[:, c] + from_core[...]

    sums = []
    for n, (dy, dx) in enumerate(group):
        target = ((y + dy) % ny) * 2 + ((x + dx) % 4) // 2
        sums.append(copy(half.at[target], from_group.at[n], to_group[n]))
        sums[-1].start()
    low = half[y * 2 + xh]
    for n, one in enumerate(sums):
        one.wait_recv()
        low = low + from_group[n]

    rows = shape_queries(low, left, right).astype(jnp.bfloat16)
    for j in range(16):
        mine[j] = rows[2 * j : 2 * j + 2]

    base, other = 8 * c, 8 * oc
    own = pl.ds(base, 8)
    swap = copy(mine.at[pl.ds(other, 8)], theirs, partner)
    swap.start()
    swap.wait_recv()
    for j in range(8):
        one, two = mine[base + j], theirs[j]
        queries[base + j, 0, xl, y, xh] = jnp.where(
            c == 0, jnp.concatenate([one, two], axis=0), jnp.concatenate([two, one], axis=0)
        )

    def send(view, peers):
        sent = [copy(view, view, peer) for peer in peers]
        for one in sent:
            one.start()
        return sent

    def arrive(sent):
        for one in sent:
            one.wait_recv()

    view = queries.reshape(16, 512, 128)
    first, second = pl.ds(base, 4), pl.ds(base + 4, 4)
    far_x, far_y = [to_x[1], to_x[0], to_x[2]], [to_y[1], to_y[0], to_y[2]]

    def start_lines(run):
        at = pl.ds(*run)
        return send(queries.at[first, at, xl, y, xh], far_x) + send(
            queries.at[second, at, xl, y, xh], far_y
        )

    def start_planes(run):
        at = pl.ds(*run)
        return send(queries.at[first, at, :, y], far_y) + send(
            queries.at[second, at, xl, :, xh], far_x
        )

    def start_swap(run):
        rows = pl.ds(64 * run[0], 64 * run[1])
        one = copy(view.at[own, rows], level.at[own, rows], partner)
        one.start()
        return [one]

    columns, lines, planes, swaps = {}, [], [], []
    for r in (4, 3, 5, 2, 6, 1, 7):
        columns[r] = copy(
            queries.at[own, 0, xl, y, xh],
            queries.at[own, REL.index(r), xl, y, xh],
            to_z[nz - r - 1],
        )
        columns[r].start()
    lines.append(start_lines(RUNS[0]))

    def next_line():
        run = RUNS[len(lines)]
        arrive([columns[r] for r in REL[run[0] : run[0] + run[1]]])
        lines.append(start_lines(run))

    def next_plane():
        arrive(lines[len(planes)])
        planes.append(start_planes(RUNS[len(planes)]))

    next_line()
    next_line()
    next_plane()
    next_line()
    next_plane()
    next_plane()
    next_plane()
    for n, run in enumerate(RUNS):
        arrive(planes[n])
        swaps.append(start_swap(run))

    def add_product(source, slab, first):
        rows = jnp.concatenate([source[slab + j] for j in range(SPAN)], axis=1)
        column = pl.ds(pl.multiple_of(slab * 128, 256), SPAN * 128)

        def tile(step, _):
            part_rows = pl.ds(pl.multiple_of(step * 256, 256), 256)
            term = lax.dot_general(
                rows, store[part_rows, column], NT, preferred_element_type=jnp.float32
            )
            for n, r in enumerate(REL):
                to = pl.ds(pl.multiple_of(64 * lax.rem(z + r, nz), 64), 64)
                block = term[64 * n : 64 * n + 64]
                if first:
                    out_ref[to, part_rows] = block
                else:
                    out_ref[to, part_rows] += block
            return 0

        lax.fori_loop(0, store.shape[0] // 256, tile, 0, unroll=6)

    load_store.wait()
    add_product(view, base, True)
    for one in swaps:
        arrive(one)
    add_product(level, other, False)
    for one in used:
        one.wait_send()


COPIES = 1 + 7 + 1 + 7 + len(RUNS) * (6 + 6 + 1)


def on_device(
    activations, out_grads, in_projection, out_projection, in_inverse, out_inverse, grad_store
):
    pairs = activations.shape[0] // (2 * SEQ)
    operands = (
        activations, out_grads, in_projection.T, out_projection.T, in_inverse, out_inverse,
        grad_store,
    )
    kern = pl.pallas_call(
        influence_kernel,
        out_shape=jax.ShapeDtypeStruct((512, grad_store.shape[0]), jnp.float32),
        in_specs=[pl.BlockSpec(memory_space=pltpu.HBM)] * len(operands),
        out_specs=pl.BlockSpec(memory_space=pltpu.VMEM),
        scratch_shapes=[
            *[pltpu.VMEM(one.shape, one.dtype) for one in operands],
            pltpu.VMEM((pairs // 2, 2, 48, 128), jnp.float32),
            pltpu.VMEM((pairs // 2, 48, 128), jnp.float32),
            pltpu.VMEM((pairs // 2, 48, 128), jnp.float32),
            pltpu.VMEM((7, 48, 128), jnp.float32),
            pltpu.VMEM((16, 2, 128), jnp.bfloat16),
            pltpu.VMEM((8, 2, 128), jnp.bfloat16),
            pltpu.VMEM((16, 8, 2, 4, 2, 4, 128), jnp.bfloat16),
            pltpu.VMEM((16, 512, 128), jnp.bfloat16),
            pltpu.SemaphoreType.DMA((len(operands),)),
            pltpu.SemaphoreType.DMA((COPIES,)),
            pltpu.SemaphoreType.DMA((COPIES,)),
        ],
        compiler_params=pltpu.CompilerParams(
            collective_id=0, has_side_effects=True, vmem_limit_bytes=32 * 1024 * 1024
        ),
    )
    return kern(*[pltpu.with_memory_space_constraint(one, pltpu.HBM) for one in operands])


def solution(mesh):
    return jax.shard_map(
        on_device,
        mesh=mesh,
        in_specs=(
            P("blk", ("grp", "wide")),
            P("blk", ("grp", "wide")),
            P(("grp", "wide"), None),
            P(("grp", "wide"), None),
            P(),
            P(),
            P(("grp", "wide", "blk"), None),
        ),
        out_specs=P(None, ("grp", "wide", "blk")),
        check_vma=False,
    )
```
